32 devices in a mesh: dp: 4 (over y, x), ctx: 4 (over z), tp: 2 (over core).
Axes of the slice: x: 2, y: 2, z: 4, core: 2. Of those that a mesh axis runs over, the one named last changes fastest.
Arguments:
- inputs: bfloat16 [4, 1024, 8192], P('dp', 'ctx', 'tp'), may hold values from -6 to 6
- cotangent: bfloat16 [4, 1024, 8192], P('dp', 'ctx', 'tp'), may hold values from -6 to 6
- residues: float32 [512, 16], P('tp'), may hold values from -3 to 3
- decay_rates: float32 [512, 16], P('tp'), may hold values from 0.0001953125 to 0.0333333333
- skip_gain: float32 [8192], P('tp'), may hold values from -1 to 1
Outputs:
- outputs: bfloat16 [4, 1024, 8192], P('dp', 'ctx', 'tp')
- grad_inputs: bfloat16 [4, 1024, 8192], P('dp', 'ctx', 'tp')
- grad_residues: float32 [512, 16], P('tp')
- grad_skip: float32 [8192], P('tp')
The draws below stay inside these ranges and needn't reach their ends.
All inputs are finite; a program needn't handle non-finite values.
Results may differ from the reference program's by a relative error of at most 0.0014.
Values sent between devices are 32-bit elements; how exact they have to be, the bound alone decides.
No kernel may reach another device: no remote copies, remote signals or barrier semaphores. Data moves between devices by JAX's collectives and lax.ppermute only.
A program may use at most 128 MiB of HBM per device.

```python
import math
import jax
import jax.numpy as jnp
from jax import lax

D = 8192
MODES = 16
BATCH = 4
SEQ = 1024
GROUPS = 512
TOKENS = 4096


def draw_decay_rates(key, part):
    key_pick, key_slow, key_fast = jax.random.split(jax.random.fold_in(key, 17), 3)
    slow_share = 0.5
    slow_pick = jax.random.uniform(key_pick, (GROUPS, MODES), dtype=jnp.float32) < slow_share
    slow_rates = jnp.exp(jax.random.uniform(key_slow, (GROUPS, MODES), dtype=jnp.float32, minval=jnp.log(0.2 / SEQ), maxval=jnp.log(2.0 / SEQ)))
    fast_rates = jnp.exp(jax.random.uniform(key_fast, (GROUPS, MODES), dtype=jnp.float32, minval=jnp.log(2.0 / SEQ), maxval=jnp.log(1.0 / 30.0)))
    return jnp.where(slow_pick, slow_rates, fast_rates).astype(jnp.float32)


def level_of(own_key, extent, shards, low, largest):
    def one(position, shards_of):
        draws = jax.random.uniform(jax.random.fold_in(jax.random.fold_in(own_key, 6), position), (shards_of,), jnp.float32, low / len(shards), largest / len(shards))
        return jnp.repeat(jnp.exp(draws), extent[position] // shards_of).reshape((-1,) + (1,) * (len(extent) - position - 1))

    level = one(*shards[0])
    for cut in shards[1:]:
        level = level * one(*cut)
    return level


def normal_values(rng, dims, spread, limit, shards=(), kind=jnp.bfloat16):
    level = level_of(rng, dims, shards, -0.22, 0.18) if shards else 1.0
    array = jax.random.normal(rng, dims, jnp.float32) * spread * level
    return jnp.minimum(jnp.maximum(array, -limit), limit).astype(kind)


def setup_inputs(seed: int = 0) -> dict:
    splits = jax.random.split(jax.random.key(seed), 6)
    return {
        "inputs": normal_values(splits[0], (BATCH, SEQ, D), 1.0, 6.0, ((0, 4), (1, 4), (2, 2))),
        "cotangent": normal_values(splits[1], (BATCH, SEQ, D), 1.0, 6.0, ((0, 4), (1, 4), (2, 2))),
        "residues": normal_values(splits[2], (GROUPS, MODES), 0.5, 3.0, ((0, 2),), jnp.float32),
        "decay_rates": draw_decay_rates(jax.random.fold_in(splits[5], 71), 0),
        "skip_gain": jnp.clip(jax.random.uniform(splits[4], (D,), jnp.float32, -1.0, 1.0) * level_of(splits[4], (D,), ((0, 2),), -0.4, 0.0), -1.0, 1.0),
    }


highest = lax.Precision.HIGHEST

def reference(inputs, cotangent, residues, decay_rates, skip_gain):
    block_rows = math.gcd(64, SEQ)
    block_count = SEQ // block_rows
    group_count, mode_count = residues.shape
    channels = inputs.shape[2]
    group_width = channels // group_count
    weight = jnp.sqrt(1.0 - jnp.exp(-2.0 * decay_rates))
    coefficient = residues * weight
    positions = jnp.arange(block_rows, dtype=jnp.float32)
    center = (block_rows - 1) / 2.0
    rate_cube = decay_rates[:, :, None]
    decay_down = jnp.exp(-rate_cube * (positions - center))
    decay_up = jnp.exp(rate_cube * (positions - center))
    from_start = jnp.exp(-rate_cube * positions)
    to_end = jnp.exp(-rate_cube * (block_rows - 1.0 - positions))
    first_weights = coefficient[:, :, None] * jnp.exp(-rate_cube * (positions + 1.0))
    last_weights = coefficient[:, :, None] * jnp.exp(-rate_cube * (block_rows - positions))
    causal_mask = positions[:, None] >= positions[None, :]
    kernel = jnp.where(causal_mask, jnp.einsum('gm,gmt,gms->gts', coefficient, decay_down, decay_up, precision=highest), 0.0)
    block_passing = jnp.exp(-decay_rates.T[:, :, None] * float(block_rows))
    skip_wide = skip_gain.reshape(group_count, group_width)
    one_step = jnp.exp(-decay_rates)

    def one_sequence(pair):
        sequence, back_row = pair
        split_x = sequence.reshape(block_count, block_rows, group_count, group_width)
        split_d = back_row.reshape(block_count, block_rows, group_count, group_width)

        def forward_turn(carried, pieces):
            state_in, grad_total = carried
            half_x, half_d = pieces
            wide_x = half_x.astype(jnp.float32)
            wide_d = half_d.astype(jnp.float32)
            local_out = jnp.einsum('gts,sgc->tgc', kernel, wide_x, precision=highest)
            carried_out = jnp.einsum('gmt,mgc->tgc', first_weights, state_in, precision=highest)
            local_back = jnp.einsum('gts,tgc->sgc', kernel, wide_d, precision=highest)
            pairs = jnp.einsum('tgc,sgc->gts', half_d, half_x, preferred_element_type=jnp.float32)
            pairs = jnp.where(causal_mask, pairs, 0.0)
            local_grad = weight * jnp.einsum('gmt,gts,gms->gm', decay_down, pairs, decay_up, precision=highest)
            start_state = jnp.einsum('gmt,tgc->mgc', from_start, wide_d, precision=highest)
            cross_grad = weight * one_step * jnp.einsum('mgc,mgc->gm', start_state, state_in, precision=highest)
            end_state = jnp.einsum('gmt,tgc->mgc', to_end, wide_x, precision=highest)
            state_out = state_in * block_passing + end_state
            return ((state_out, grad_total + local_grad + cross_grad), (local_out + carried_out + skip_wide * wide_x, local_back + skip_wide * wide_d, start_state))
        empty_state = jnp.zeros((mode_count, group_count, group_width), jnp.float32)
        empty_grad = jnp.zeros((group_count, mode_count), jnp.float32)
        final_pair, stacked = lax.scan(forward_turn, (empty_state, empty_grad), (split_x, split_d))
        forward_out, backward_local, start_states = stacked

        def backward_turn(carried, local_start):
            return (carried * block_passing + local_start, carried)
        final_state, after_states = lax.scan(backward_turn, empty_state, start_states, reverse=True)
        carried_back = jnp.einsum('gmt,kmgc->ktgc', last_weights, after_states, precision=highest)
        result_out = forward_out.reshape(SEQ, channels).astype(jnp.bfloat16)
        result_back = (backward_local + carried_back).reshape(SEQ, channels).astype(jnp.bfloat16)
        return (result_out, result_back, final_pair[1])
    outputs, grad_inputs, grad_parts = lax.map(one_sequence, (inputs, cotangent))
    scale = 1.0 / math.sqrt(TOKENS)
    grad_residues = lax.optimization_barrier(jnp.sum(grad_parts, axis=0)) * scale
    grad_skip = jnp.einsum('btc,btc->c', inputs.astype(jnp.float32), cotangent.astype(jnp.float32), precision=highest) * scale
    return (outputs, grad_inputs, grad_residues, grad_skip)
```

```python
import functools
import math

import jax
import jax.numpy as jnp
from jax import lax
from jax.experimental import pallas as pl
from jax.experimental.pallas import tpu as pltpu
from jax.sharding import PartitionSpec as P


f32 = jnp.float32
bf16 = jnp.bfloat16
LANES = 128


def split(value):
    high = value.astype(bf16)
    low = (value - high.astype(f32)).astype(bf16)
    return high, low


def mm(left, right):
    return lax.dot_general(left, right, (((1,), (0,)), ((), ())), preferred_element_type=f32)


def iota(shape, axis):
    return lax.broadcasted_iota(jnp.int32, shape, axis)


def column_of(row):
    return jnp.broadcast_to(row, (LANES, LANES)).T


def ends_kernel(width, modes, tiles, x_ref, d_ref, rate_ref, ex_ref, ed_ref):
    rows = x_ref.shape[0]
    per_tile = LANES // width
    owner = iota((modes, LANES), 1) // width
    spot = iota((LANES, LANES), 1).astype(f32)
    for k in range(tiles):
        lanes = slice(k * LANES, (k + 1) * LANES)
        rate = column_of(rate_ref[:, lanes])
        late = jnp.exp(-rate * (LANES - 1.0 - spot))
        early = jnp.exp(-rate * spot)
        step = jnp.exp(-rate * float(LANES))
        late_parts, early_parts = [late], [early]
        for _ in range(rows // LANES - 1):
            late_parts.insert(0, late_parts[0] * step)
            early_parts.append(early_parts[-1] * step)
        for table, src, dst in ((late_parts, x_ref, ex_ref), (early_parts, d_ref, ed_ref)):
            high, low = split(jnp.concatenate(table, axis=1))
            block = src[:, lanes]
            full = mm(high, block) + mm(low, block)
            total = full[0:modes]
            for g in range(1, per_tile):
                total = jnp.where(owner == g, full[g * modes : (g + 1) * modes], total)
            dst[:, lanes] = total


def swap_blocks(parts, width):
    count = len(parts)
    lane = iota(parts[0].shape, 1)
    bit = 1
    while bit < count:
        odd = (lane // (width * bit)) % 2 == 1
        fresh = [None] * count
        for j in range(count):
            if j & bit == 0:
                other = j | bit
                fresh[j] = jnp.where(odd, pltpu.roll(parts[other], width * bit, 1), parts[j])
                fresh[other] = jnp.where(odd, parts[other], pltpu.roll(parts[j], LANES - width * bit, 1))
        parts = fresh
        bit *= 2
    return parts


def to_chunks(block, width, chunk):
    count = LANES // width
    wide = block.astype(f32)
    halves = []
    for h in range(block.shape[0] // (chunk * count)):
        base = h * chunk * count
        parts = [wide[base + j * chunk : base + (j + 1) * chunk] for j in range(count)]
        halves.append(jnp.concatenate(swap_blocks(parts, width), axis=0))
    return jnp.concatenate(halves, axis=1)


def from_chunks(value, width, chunk):
    count = LANES // width
    out = []
    for h in range(value.shape[1] // LANES):
        lanes = slice(h * LANES, (h + 1) * LANES)
        parts = [value[g * chunk : (g + 1) * chunk, lanes] for g in range(count)]
        out.extend(swap_blocks(parts, width))
    return jnp.concatenate(out, axis=0)


def local_kernel(
    width, modes, tiles, x_ref, d_ref, rate_ref, coef_ref, skip_ref, yx_ref, yd_ref, grad_ref, gskip_ref, tri_ref
):
    rows = x_ref.shape[0]
    chunk = modes
    count = rows // chunk
    span = count * width
    middle = (count - 1) / 2.0

    @pl.when(pl.program_id(0) == 0)
    def _():
        r, c = iota((span, span), 0), iota((span, span), 1)
        same = (r % width) == (c % width)
        tri_ref[0] = (same & (r // width < c // width)).astype(bf16)
        tri_ref[1] = (same & (r // width > c // width)).astype(bf16)

    sq = (LANES, LANES)
    r, c = iota(sq, 0), iota(sq, 1)
    own = (r // chunk) == (c // chunk)
    r_spot, c_spot = (r % chunk).astype(f32), (c % chunk).astype(f32)
    causal = own & (r % chunk >= c % chunk)
    hop = (iota((LANES, span), 1) // width).astype(f32) - middle
    for k in range(tiles):
        lanes = slice(k * LANES, (k + 1) * LANES)
        rate_row = rate_ref[:, lanes]
        coef_row = coef_ref[:, lanes]
        rate = column_of(rate_row)
        start_t = jnp.where(own, jnp.exp(-rate * c_spot), 0.0)
        end_t = jnp.where(own, jnp.exp(-rate * (chunk - 1.0 - c_spot)), 0.0)
        down = jnp.where(own, jnp.exp(-rate_row * r_spot), 0.0)
        up = jnp.where(own, jnp.exp(rate_row * r_spot), 0.0)
        first = down * (coef_row * jnp.exp(rate_row * (chunk - 1.0)))
        last = up * coef_row
        first_h, first_l = split(first)
        last_h, last_l = split(last)
        end_h, end_l = split(end_t)
        start_h, start_l = split(start_t)
        up_h, up_l = split(up)
        first_hl = jnp.concatenate([first_h, first_l], axis=1)
        last_hl = jnp.concatenate([last_h, last_l], axis=1)
        toeplitz = mm(first_hl, jnp.concatenate([end_h, end_h], axis=0)) + mm(first_h, end_l)
        toeplitz = jnp.where(causal, toeplitz, 0.0)
        rate_wide = jnp.concatenate([rate] * (span // LANES), axis=1)
        grow = jnp.exp(rate_wide * (chunk * hop))
        fade = jnp.exp(-rate_wide * (chunk * hop))
        x_nat, d_nat = x_ref[:, lanes], d_ref[:, lanes]
        x_two = to_chunks(x_nat, width, chunk).astype(bf16)
        d_two = to_chunks(d_nat, width, chunk).astype(bf16)

        def direction(kernel, ends_h, ends_l, data, scale_in, scale_out, tri, carry_hl, carry_h):
            k_h, k_l = split(kernel)
            left = jnp.concatenate(
                [jnp.concatenate([k_h, k_l], axis=1), jnp.concatenate([ends_h, ends_l], axis=1)], axis=0
            )
            both = mm(left, jnp.concatenate([data, data], axis=0))
            out, ends = both[:LANES], both[LANES:]
            e_h, e_l = split(ends * scale_in)
            moved = mm(e_h, tri) + mm(e_l, tri)
            state = moved * scale_out
            s_h, s_l = split(state)
            out = out + mm(carry_hl, jnp.concatenate([s_h, s_h], axis=0)) + mm(carry_h, s_l)
            return out, ends, state

        out_x, _, state_x = direction(toeplitz, end_h, end_l, x_two, grow, fade, tri_ref[0], first_hl, first_h)
        out_d, starts_d, _ = direction(toeplitz.T, start_h, start_l, d_two, fade, grow, tri_ref[1], last_hl, last_h)
        x_wide, d_wide = x_nat.astype(f32), d_nat.astype(f32)
        skip = skip_ref[:, lanes]
        yx_ref[:, lanes] = from_chunks(out_x, width, chunk) + skip * x_wide
        yd_ref[:, lanes] = from_chunks(out_d, width, chunk) + skip * d_wide
        gskip_ref[:, lanes] = jnp.sum(x_wide * d_wide, axis=0, keepdims=True)
        pairs = lax.dot_general(d_two, x_two, (((1,), (1,)), ((), ())), preferred_element_type=f32)
        p_h, p_l = split(jnp.where(causal, pairs, 0.0))
        near = mm(jnp.concatenate([p_h, p_l], axis=1), jnp.concatenate([up_h, up_h], axis=0)) + mm(p_h, up_l)
        near = jnp.sum(near * down, axis=0, keepdims=True)
        far = starts_d * state_x
        folded = far[:, :LANES]
        for h in range(1, span // LANES):
            folded = folded + far[:, h * LANES : (h + 1) * LANES]
        far = jnp.sum(folded.T, axis=0, keepdims=True) * jnp.exp(rate_row * (chunk - 1.0))
        grad_ref[:, lanes] = near + far


def carry_grad_kernel(width, modes, state_ref, start_ref, rate_ref, near_ref, weight_ref, skip_ref, scale_ref, out_ref):
    total = state_ref.shape[1]
    sq = (LANES, LANES)
    same = ((iota(sq, 0) // width) == (iota(sq, 1) // width)).astype(bf16)
    pick = iota((modes, LANES), 0) == iota((modes, LANES), 1) % modes
    for k in range(total // LANES):
        lanes = slice(k * LANES, (k + 1) * LANES)
        high, low = split(state_ref[:, lanes] * start_ref[:, lanes])
        sums = mm(high, same) + mm(low, same)
        far = jnp.sum(jnp.where(pick, sums, 0.0), axis=0, keepdims=True)
        rate = rate_ref[:, lanes]
        out_ref[0:1, lanes] = (near_ref[:, lanes] + far * jnp.exp(-rate)) * (weight_ref[:, lanes] * scale_ref[0, 0])
        out_ref[1:2, lanes] = skip_ref[:, lanes] * scale_ref[0, 0]


def finish_kernel(width, modes, wide, tiles, yx_ref, yd_ref, sx_ref, sd_ref, rate_ref, coef_ref, ox_ref, od_ref):
    rows = yx_ref.shape[0]
    groups = wide // width
    mask = (iota((wide, wide), 0) // modes) == (iota((wide, wide), 1) // width)
    for k in range(tiles):
        lanes = slice(k * wide, (k + 1) * wide)
        rate = rate_ref[:, lanes]
        coef = coef_ref[:, lanes]
        spot = iota((8, wide), 0).astype(f32)
        first = coef * jnp.exp(-rate * (spot + 1.0))
        last = coef * jnp.exp(-rate * (8.0 - spot))
        size = 8
        while size < rows:
            step = jnp.exp(-rate * float(size))
            first = jnp.concatenate([first, first * step], axis=0)
            last = jnp.concatenate([last * step, last], axis=0)
            size *= 2
        for table, s_ref, y_ref, o_ref in ((first, sx_ref, yx_ref, ox_ref), (last, sd_ref, yd_ref, od_ref)):
            t_h, t_l = split(table)
            s_h, s_l = split(s_ref[:, lanes])
            zero = jnp.zeros((), bf16)
            b_h = jnp.where(mask, jnp.concatenate([s_h] * groups, axis=0), zero)
            b_l = jnp.where(mask, jnp.concatenate([s_l] * groups, axis=0), zero)
            total = y_ref[:, lanes] + mm(t_h, b_h) + mm(t_l, b_h) + mm(t_h, b_l)
            o_ref[:, lanes] = total.astype(bf16)


def shards(inputs, cotangent, residues, decay_rates, skip_gain):
    local_batch, rows, channels = inputs.shape
    group_count, modes = residues.shape
    width = channels // group_count
    x, d = inputs.reshape(local_batch * rows, channels), cotangent.reshape(local_batch * rows, channels)
    weight = jnp.sqrt(1.0 - jnp.exp(-2.0 * decay_rates)).reshape(1, channels)
    coef = residues.reshape(1, channels) * weight
    rate = decay_rates.reshape(1, channels)
    skip = skip_gain.reshape(1, channels)
    count = lax.axis_size("ctx")

    tiles = math.gcd(4, channels // LANES)
    step = tiles * LANES
    steps = channels // step
    data = pl.BlockSpec((rows, step), lambda i: (0, i))
    state = pl.BlockSpec((modes, step), lambda i: (0, i))
    line = pl.BlockSpec((1, step), lambda i: (0, i))
    end_x, start_d = pl.pallas_call(
        functools.partial(ends_kernel, width, modes, tiles),
        grid=(steps,),
        in_specs=[data, data, line],
        out_specs=[state, state],
        out_shape=[jax.ShapeDtypeStruct((modes, channels), f32)] * 2,
        name="ends",
    )(x, d, rate)

    fade = jnp.exp(-decay_rates * float(rows)).T
    fade = jnp.repeat(fade, width, axis=1)

    before, after = end_x, start_d
    have_x, have_d = None, None
    distance = 1
    power, prior = fade, None
    while distance < count:
        up = [(i, i + distance) for i in range(count - distance)]
        dn = [(i + distance, i) for i in range(count - distance)]
        got_x = lax.ppermute(before, "ctx", up)
        got_d = lax.ppermute(after, "ctx", dn)
        if have_x is None:
            have_x, have_d = got_x, got_d
        else:
            have_x, have_d = have_x + prior * got_x, have_d + prior * got_d
        prior = power if prior is None else prior * power
        if distance * 2 < count:
            before, after = before + power * got_x, after + power * got_d
            power = power * power
        distance *= 2

    tiles_b = math.gcd(2, channels // LANES)
    step_b = tiles_b * LANES
    data_b = pl.BlockSpec((rows, step_b), lambda i: (0, i))
    line_b = pl.BlockSpec((1, step_b), lambda i: (0, i))
    span = rows // modes * width
    y_x, y_d, near, near_skip = pl.pallas_call(
        functools.partial(local_kernel, width, modes, tiles_b),
        grid=(channels // step_b,),
        in_specs=[data_b, data_b, line_b, line_b, line_b],
        out_specs=[data_b, data_b, line_b, line_b],
        out_shape=[jax.ShapeDtypeStruct((rows, channels), f32)] * 2 + [jax.ShapeDtypeStruct((1, channels), f32)] * 2,
        scratch_shapes=[pltpu.VMEM((2, span, span), bf16)],
        name="local",
    )(x, d, rate, coef, skip)

    token_total = local_batch * rows * lax.axis_size("dp") * count
    scale = jnp.full((1, 1), 1.0 / math.sqrt(token_total), f32)
    grads = pl.pallas_call(
        functools.partial(carry_grad_kernel, width, modes),
        in_specs=[pl.BlockSpec(memory_space=pltpu.VMEM)] * 6 + [pl.BlockSpec(memory_space=pltpu.SMEM)],
        out_shape=jax.ShapeDtypeStruct((2, channels), f32),
        name="carry_grad",
    )(have_x, start_d, rate, near, weight, near_skip, scale)
    for axis in ("dp", "ctx"):
        size = lax.axis_size(axis)
        total = grads
        for k in range(1, size):
            total = total + lax.ppermute(grads, axis, [(i, (i + k) % size) for i in range(size)])
        grads = total

    wide = min(256, channels)
    tiles_c = math.gcd(2, channels // wide)
    step_c = tiles_c * wide
    data_c = pl.BlockSpec((rows, step_c), lambda i: (0, i))
    state_c = pl.BlockSpec((modes, step_c), lambda i: (0, i))
    line_c = pl.BlockSpec((1, step_c), lambda i: (0, i))
    out, back = pl.pallas_call(
        functools.partial(finish_kernel, width, modes, wide, tiles_c),
        grid=(channels // step_c,),
        in_specs=[data_c, data_c, state_c, state_c, line_c, line_c],
        out_specs=[data_c, data_c],
        out_shape=[jax.ShapeDtypeStruct((rows, channels), bf16)] * 2,
        name="finish",
    )(y_x, y_d, have_x, have_d, rate, coef)
    return (
        out.reshape(inputs.shape),
        back.reshape(inputs.shape),
        grads[0].reshape(group_count, modes),
        grads[1],
    )


def solution(mesh):
    placed = (P("dp", "ctx", "tp"), P("dp", "ctx", "tp"), P("tp", None), P("tp", None), P("tp"))
    return jax.shard_map(
        shards,
        mesh=mesh,
        in_specs=placed,
        out_specs=(P("dp", "ctx", "tp"), P("dp", "ctx", "tp"), P("tp", None), P("tp")),
        check_vma=False,
    )
```

```python
import functools
import math

import jax
import jax.numpy as jnp
from jax import lax
from jax.experimental import pallas as pl
from jax.experimental.pallas import tpu as pltpu
from jax.sharding import PartitionSpec as P


f32 = jnp.float32
bf16 = jnp.bfloat16
LANES = 128
TILES_A, TILES_B, TILES_C = 8, 2, 8
VMEM_LIMIT = 24 * 2**20
CUTS = (6, 11)


def split(value):
    high = value.astype(bf16)
    low = (value - high.astype(f32)).astype(bf16)
    return high, low


def mm(left, right):
    return lax.dot_general(left, right, (((1,), (0,)), ((), ())), preferred_element_type=f32)


def iota(shape, axis):
    return lax.broadcasted_iota(jnp.int32, shape, axis)


def sel_rows(full, block, owner):
    total = full[0:block]
    for g in range(1, full.shape[0] // block):
        total = jnp.where(owner == g, full[g * block : (g + 1) * block], total)
    return total


def stack(parts, axis):
    return jnp.concatenate(parts, axis=axis)


def column(row, eye):
    return jnp.sum(jnp.where(eye, row, 0.0), axis=1, keepdims=True)


def ends_kernel(width, modes, tiles, x_ref, d_ref, rate_ref, near_ref, far_ref, wide_ref):
    rows = x_ref.shape[0]
    sq = (LANES, LANES)
    eye = iota(sq, 0) == iota(sq, 1)
    same = (iota(sq, 0) // width == iota(sq, 1) // width).astype(bf16)
    owner = iota((modes, LANES), 1) // width
    pick = iota((modes, LANES), 0) == iota((modes, LANES), 1) % width
    spot = iota(sq, 1).astype(f32)
    even = lax.axis_index("ctx") % 2 == 0
    pieces = rows // LANES
    for k in range(tiles):
        lanes = slice(k * LANES, (k + 1) * LANES)
        row = rate_ref[:, lanes]
        rate = column(row, eye)
        spread = jnp.where(pick, row, 0.0)
        a = spread.astype(bf16)
        b = (spread - a.astype(f32)).astype(bf16)
        c = (spread - a.astype(f32) - b.astype(f32)).astype(bf16)
        rate_wide = mm(a, same) + mm(b, same) + mm(c, same)
        wide_ref[:, lanes] = rate_wide
        step = jnp.exp(-rate_wide * float(LANES))
        got = []
        for power, src in ((LANES - 1.0 - spot, x_ref), (spot, d_ref)):
            high, low = split(jnp.exp(-rate * power))
            flat = stack([src[h * LANES : (h + 1) * LANES, lanes] for h in range(pieces)], 1)
            full = mm(stack([high, low], 1), stack([flat, flat], 0))
            got.append([sel_rows(full[:, h * LANES : (h + 1) * LANES], modes, owner) for h in range(pieces)])
        end = got[0][0]
        for h in range(1, pieces):
            end = end * step + got[0][h]
        start = got[1][pieces - 1]
        for h in range(pieces - 2, -1, -1):
            start = start * step + got[1][h]
        near_ref[:, lanes] = jnp.where(even, end, start)
        far_ref[:, lanes] = jnp.where(even, start, end)


def local_kernel(width, modes, tiles, *refs):
    x_ref, d_ref, rate_ref, wide_ref, coef_ref, skip_ref = refs[:6]
    yx_ref, yd_ref, grad_ref, far_ref, gskip_ref, own_ref = refs[-6:]
    rows = x_ref.shape[0]
    groups = LANES // width
    fold = max(1, 2 * LANES // (groups * modes))
    chunk = fold * modes
    count = rows // chunk
    sq = (LANES, LANES)

    @pl.when(pl.program_id(0) == 0)
    def _():
        own_ref[...] = ((iota(sq, 0) // modes) == (iota(sq, 1) // width)).astype(bf16)

    own = own_ref[...]
    owner = iota((chunk, LANES), 1) // width
    flat = (chunk, fold * LANES)
    t_int = iota(flat, 0)
    s_int = iota(flat, 1) // LANES * modes + iota(flat, 1) % modes
    spot = iota((chunk, LANES), 0).astype(f32)
    place = iota((modes, LANES), 1) % modes

    def spread(compact):
        return stack([compact] * groups, 0) * own

    def tall(compact):
        return stack([spread(compact[f * modes : (f + 1) * modes]) for f in range(fold)], 0)

    def broad(compact):
        return stack([spread(compact[:, f * LANES : (f + 1) * LANES]) for f in range(fold)], 1)

    def halves(value, size):
        return value[:size] + value[size:]

    def three(table_h, table_l, right_h, right_l):
        left = stack([stack([table_h, table_h], 1), stack([table_l, jnp.zeros_like(table_l)], 1)], 0)
        return halves(mm(left, stack([right_h, right_l], 0)), table_h.shape[0])

    for k in range(tiles):
        lanes = slice(k * LANES, (k + 1) * LANES)
        row, coef, wide = rate_ref[:, lanes], coef_ref[:, lanes], wide_ref[:, lanes]
        skip = skip_ref[:, lanes]
        leap = jnp.exp(-wide * float(chunk))
        down = jnp.exp(-row * spot)
        up = jnp.exp(row * spot)
        up_h, up_l = split(up)
        first_h, first_l = split(down * (coef * jnp.exp(row * (chunk - 1.0))))
        last_h, last_l = split(up * coef)
        start = stack([jnp.exp(-wide * (place + f * modes).astype(f32)) for f in range(fold)], 1)
        end = stack([jnp.exp(-wide * (chunk - 1 - f * modes - place).astype(f32)) for f in range(fold)], 1)
        start_h, start_l = split(start)
        end_h, end_l = split(end)
        forth = jnp.where(t_int >= s_int, three(first_h, first_l, broad(end_h), broad(end_l)), 0.0)
        back = jnp.where(t_int <= s_int, three(last_h, last_l, broad(start_h), broad(start_l)), 0.0)

        def tiles_of(src):
            expanded = [tall(src[j * chunk : (j + 1) * chunk, lanes]) for j in range(count)]
            return [stack(expanded[j : j + 2], 1) for j in range(0, count, 2)]

        def near_part(kernel, ends_h, ends_l, right, src, dst):
            k_h, k_l = split(kernel)
            left = stack([k_h, k_l, ends_h, ends_l], 0)
            found = []
            for p, block in enumerate(right):
                res = mm(left, block)
                own_part = halves(res[: 2 * chunk], chunk)
                ends = halves(res[2 * chunk :], modes)
                for q in range(2):
                    half = slice(q * LANES, (q + 1) * LANES)
                    spots = slice((2 * p + q) * chunk, (2 * p + q + 1) * chunk)
                    dst[spots, lanes] = own_part[:, half] + skip * src[spots, lanes].astype(f32)
                    found.append(ends[:, half])
            return found

        def far_part(table_h, table_l, states, dst):
            for p in range(0, count, 2):
                pair = [split(states[p + q]) for q in range(2)]
                res = three(
                    table_h,
                    table_l,
                    stack([spread(h) for h, _ in pair], 1),
                    stack([spread(l) for _, l in pair], 1),
                )
                for q in range(2):
                    spots = slice((p + q) * chunk, (p + q + 1) * chunk)
                    dst[spots, lanes] += res[:, q * LANES : (q + 1) * LANES]

        x_right = tiles_of(x_ref)
        ends_x = near_part(forth, end_h, end_l, x_right, x_ref, yx_ref)
        pairs = lax.dot_general(
            stack([d_ref[j * chunk : (j + 1) * chunk, lanes] for j in range(count)], 1),
            stack(x_right, 1),
            (((1,), (1,)), ((), ())),
            preferred_element_type=f32,
        )
        starts_d = near_part(back, start_h, start_l, tiles_of(d_ref), d_ref, yd_ref)
        state = jnp.zeros((modes, LANES), f32)
        states = []
        far = state
        for j in range(count):
            states.append(state)
            far = far + starts_d[j] * state
            state = (state + ends_x[j]) * leap
        far_ref[:, lanes] = far * jnp.exp(wide * float(chunk))
        far_part(first_h, first_l, states, yx_ref)
        state = jnp.zeros((modes, LANES), f32)
        states = [None] * count
        for j in range(count - 1, -1, -1):
            states[j] = state
            state = (state + starts_d[j]) * leap
        far_part(last_h, last_l, states, yd_ref)
        p_h, p_l = split(jnp.where(t_int >= s_int, pairs, 0.0))
        res = mm(stack([p_h, p_l], 0), stack([tall(up_h), tall(up_l)], 1))
        near = res[:chunk, :LANES] + res[:chunk, LANES:] + res[chunk:, :LANES]
        grad_ref[:, lanes] = jnp.sum(near * down, axis=0, keepdims=True)
        total = jnp.zeros((chunk, LANES), f32)
        for j in range(count):
            spots = slice(j * chunk, (j + 1) * chunk)
            total = total + x_ref[spots, lanes].astype(f32) * d_ref[spots, lanes].astype(f32)
        gskip_ref[:, lanes] = jnp.sum(total, axis=0, keepdims=True)


def carry_grad_kernel(width, modes, scale, four, *refs):
    out_ref = refs[-1]
    near_ref, far_ref, rate_ref, weight_ref, skip_ref = refs[:5]
    p_ref, q_ref = refs[5:7]
    sq = (LANES, LANES)
    same = ((iota(sq, 0) // width) == (iota(sq, 1) // width)).astype(bf16)
    pick = iota((modes, LANES), 0) == iota((modes, LANES), 1) % modes
    place = lax.axis_index("ctx")
    inner = ((place == 1) | (place == 2)).astype(f32)
    middle = (place == 1).astype(f32)
    for k in range(p_ref.shape[1] // LANES):
        lanes = slice(k * LANES, (k + 1) * LANES)
        value = p_ref[:, lanes] * q_ref[:, lanes]
        if four:
            r_ref, s_ref = refs[7:9]
            value = value * inner + r_ref[:, lanes] * s_ref[:, lanes] * middle
        high, low = split(value + far_ref[:, lanes])
        sums = mm(stack([high, low], 1), stack([same, same], 0))
        far = jnp.sum(jnp.where(pick, sums, 0.0), axis=0, keepdims=True)
        out_ref[0:1, lanes] = (near_ref[:, lanes] + far * jnp.exp(-rate_ref[:, lanes])) * (weight_ref[:, lanes] * scale)
        out_ref[1:2, lanes] = skip_ref[:, lanes] * scale


def finish_kernel(width, modes, tiles, forward, four, y_ref, rate_ref, wide_ref, coef_ref, *refs):
    o_ref = refs[-1]
    rows = y_ref.shape[0]
    groups = LANES // width
    sq = (LANES, LANES)
    own = ((iota(sq, 0) // modes) == (iota(sq, 1) // width)).astype(bf16)
    spot = iota((8, LANES), 0).astype(f32)
    pieces = rows // LANES
    place = lax.axis_index("ctx")
    if not forward:
        place = 3 - place
    for k in range(tiles):
        lanes = slice(k * LANES, (k + 1) * LANES)
        rate, coef, wide = rate_ref[:, lanes], coef_ref[:, lanes], wide_ref[:, lanes]
        state = refs[0][:, lanes]
        if four:
            both = state + refs[2][:, lanes] * jnp.exp(-wide * float(rows))
            state = jnp.where(place == 0, 0.0, jnp.where(place == 2, refs[1][:, lanes], both))
        step = jnp.exp(-wide * float(LANES))
        table = coef * jnp.exp(-rate * (spot + 1.0 if forward else 8.0 - spot))
        size = 8
        while size < LANES:
            more = table * jnp.exp(-rate * float(size))
            table = stack([table, more] if forward else [more, table], 0)
            size *= 2
        t_h, t_l = split(table)
        highs, lows = [], []
        for _ in range(pieces):
            s_h, s_l = split(state)
            highs.append(stack([s_h] * groups, 0) * own)
            lows.append(stack([s_l] * groups, 0) * own)
            state = state * step
        if not forward:
            highs, lows = highs[::-1], lows[::-1]
        high, low = stack(highs, 1), stack(lows, 1)
        total = mm(stack([t_h, t_l], 1), stack([high, high], 0)) + mm(t_h, low)
        for h in range(pieces):
            spots = slice(h * LANES, (h + 1) * LANES)
            o_ref[spots, lanes] = (y_ref[spots, lanes] + total[:, spots]).astype(bf16)


def swap_states(near, far, power, even, count):
    end, start = jnp.where(even, near, far), jnp.where(even, far, near)
    before, after, prior, distance = end, start, None, 1
    have_x, have_d = None, None
    while distance < count:
        got_x = lax.ppermute(before, "ctx", [(i, i + distance) for i in range(count - distance)])
        got_d = lax.ppermute(after, "ctx", [(i + distance, i) for i in range(count - distance)])
        have_x = got_x if prior is None else have_x + prior * got_x
        have_d = got_d if prior is None else have_d + prior * got_d
        prior = power if prior is None else prior * power
        before, after = before + power * got_x, after + power * got_d
        power = power * power
        distance *= 2
    return have_x, have_d, start


def layer(inputs, cotangent, residues, decay_rates, skip_gain):
    local_batch, rows, channels = inputs.shape
    group_count, modes = residues.shape
    width = channels // group_count
    x, d = inputs.reshape(local_batch * rows, channels), cotangent.reshape(local_batch * rows, channels)
    rate = decay_rates.reshape(1, channels)
    weight = jnp.sqrt(1.0 - jnp.exp(-2.0 * rate))
    coef = residues.reshape(1, channels) * weight
    skip = skip_gain.reshape(1, channels)
    count = lax.axis_size("ctx")
    four = count == 4
    blocks = channels // LANES
    every = pl.BlockSpec(memory_space=pl.ANY)
    params = pltpu.CompilerParams(vmem_limit_bytes=VMEM_LIMIT)

    def specs(tiles, offset=0):
        step = tiles * LANES
        index = lambda i: (0, i + offset)
        return pl.BlockSpec((rows, step), index), pl.BlockSpec((modes, step), index), pl.BlockSpec((1, step), index)

    tiles = math.gcd(TILES_A, blocks)
    data, state, line = specs(tiles)
    near, far, wide = pl.pallas_call(
        functools.partial(ends_kernel, width, modes, tiles),
        grid=(blocks // tiles,),
        in_specs=[data, data, line],
        out_specs=[state, state, state],
        out_shape=[jax.ShapeDtypeStruct((modes, channels), f32)] * 3,
        compiler_params=params,
        name="ends",
    )(x, d, rate)
    power = jnp.exp(-wide * float(rows))

    tiles_b = math.gcd(TILES_B, blocks)
    steps = blocks // tiles_b

    def local(first, size, past):
        data, state, line = specs(tiles_b, first)
        return pl.pallas_call(
            functools.partial(local_kernel, width, modes, tiles_b),
            grid=(size,),
            in_specs=[data, data, line, state, line, line] + ([] if past is None else [every] * 5),
            out_specs=[data, data, line, state, line],
            out_shape=[jax.ShapeDtypeStruct((rows, channels), f32)] * 2
            + [jax.ShapeDtypeStruct((size_of, channels), f32) for size_of in (1, modes, 1)],
            scratch_shapes=[pltpu.VMEM((LANES, LANES), bf16)],
            input_output_aliases={} if past is None else {6 + n: n for n in range(5)},
            compiler_params=params,
            name="local",
        )(x, d, rate, wide, coef, skip, *(past or ()))

    def swap(value, pairs):
        return lax.ppermute(value, "ctx", pairs)

    if four:
        one = swap(near, [(0, 1), (1, 0), (2, 3), (3, 2)])
        cut_a, cut_b = max(1, steps * CUTS[0] // 16), max(2, steps * CUTS[1] // 16)
        past = local(0, cut_a, None)
        meet = far + power * one
        past, meet = lax.optimization_barrier((past, meet))
        two = swap(meet, [(1, 2), (2, 1)])
        past = local(cut_a, cut_b - cut_a, past)
        past, two = lax.optimization_barrier((past, two))
        three = swap(two, [(1, 0), (2, 3)])
        y_x, y_d, grad, far_grad, gskip = local(cut_b, steps - cut_b, past)
        states_x = states_d = (one, two, three)
        factors = (one, near, meet, two)
    else:
        even = lax.axis_index("ctx") % 2 == 0
        have_x, have_d, start = swap_states(near, far, power, even, count)
        y_x, y_d, grad, far_grad, gskip = local(0, steps, None)
        states_x, states_d = (have_x,), (have_d,)
        factors = (have_x, start)

    token_total = local_batch * rows * lax.axis_size("dp") * count
    grads = pl.pallas_call(
        functools.partial(carry_grad_kernel, width, modes, 1.0 / math.sqrt(token_total), four),
        in_specs=[pl.BlockSpec(memory_space=pltpu.VMEM)] * (5 + len(factors)),
        out_shape=jax.ShapeDtypeStruct((2, channels), f32),
        compiler_params=params,
        name="carry_grad",
    )(grad, far_grad, rate, weight, gskip, *factors)

    tiles_c = math.gcd(TILES_C, blocks)
    steps = blocks // tiles_c

    def finish(forward, first, size, past):
        data, state, line = specs(tiles_c, first)
        y, states = (y_x, states_x) if forward else (y_d, states_d)
        return pl.pallas_call(
            functools.partial(finish_kernel, width, modes, tiles_c, forward, four),
            grid=(size,),
            in_specs=[data, line, state, line] + [state] * len(states) + ([] if past is None else [every]),
            out_specs=data,
            out_shape=jax.ShapeDtypeStruct((rows, channels), bf16),
            input_output_aliases={} if past is None else {4 + len(states): 0},
            compiler_params=params,
            name="finish",
        )(y, rate, wide, coef, *states, *(() if past is None else (past,)))

    results = {True: None, False: None}
    queue = [(True, 0, steps // 2), (True, steps // 2, steps - steps // 2)]
    queue += [(False, 0, steps // 2), (False, steps // 2, steps - steps // 2)]
    queue = [piece for piece in queue if piece[2] > 0]
    rounds = [("dp", k) for k in doubling(lax.axis_size("dp"))] + [("ctx", k) for k in doubling(count)]
    for axis, k in rounds:
        other = lax.ppermute(grads, axis, [(i, i ^ k) for i in range(lax.axis_size(axis))])
        if queue:
            forward, first, size = queue.pop(0)
            results[forward] = finish(forward, first, size, results[forward])
            results[forward], other = lax.optimization_barrier((results[forward], other))
        grads = grads + other
    for forward, first, size in queue:
        results[forward] = finish(forward, first, size, results[forward])
    return (
        results[True].reshape(inputs.shape),
        results[False].reshape(inputs.shape),
        grads[0].reshape(group_count, modes),
        grads[1],
    )


def doubling(size):
    return [1 << n for n in range(size.bit_length() - 1)]


def solution(mesh):
    placed = (P("dp", "ctx", "tp"), P("dp", "ctx", "tp"), P("tp", None), P("tp", None), P("tp"))
    return jax.shard_map(
        layer,
        mesh=mesh,
        in_specs=placed,
        out_specs=(P("dp", "ctx", "tp"), P("dp", "ctx", "tp"), P("tp", None), P("tp")),
        check_vma=False,
    )
```

```python
import functools
import math

import jax
import jax.numpy as jnp
from jax import lax
from jax.experimental import pallas as pl
from jax.experimental.pallas import tpu as pltpu
from jax.sharding import PartitionSpec as P


f32 = jnp.float32
bf16 = jnp.bfloat16
LANES = 128
TILES_A, TILES_B, TILES_C = 8, 4, 8
VMEM_LIMIT = 16 * 2**20
CUTS = (6, 12)


def split(value):
    high = value.astype(bf16)
    low = (value - high.astype(f32)).astype(bf16)
    return high, low


def mm(left, right):
    return lax.dot_general(left, right, (((1,), (0,)), ((), ())), preferred_element_type=f32)


def iota(shape, axis):
    return lax.broadcasted_iota(jnp.int32, shape, axis)


def lanes_of(k, tiles, first=0):
    return pl.ds(pl.multiple_of((pl.program_id(0) + first) * (tiles * LANES) + k * LANES, LANES), LANES)


def sel_rows(full, block, owner):
    total = full[0:block]
    for g in range(1, full.shape[0] // block):
        total = jnp.where(owner == g, full[g * block : (g + 1) * block], total)
    return total


def stack(parts, axis):
    return jnp.concatenate(parts, axis=axis)


def column(row, eye):
    return jnp.sum(jnp.where(eye, row, 0.0), axis=1, keepdims=True)


def halves(value, size):
    return value[:size] + value[size:]


def three(table_h, table_l, right_h, right_l):
    left = stack([stack([table_h, table_h], 1), stack([table_l, jnp.zeros_like(table_l)], 1)], 0)
    return halves(mm(left, stack([right_h, right_l], 0)), table_h.shape[0])


def chunk_of(width, modes):
    return max(1, 2 * width // modes) * modes


def block_mask(width, modes):
    sq = (LANES, LANES)
    return ((iota(sq, 0) // modes) == (iota(sq, 1) // width)).astype(bf16)


def ends_kernel(width, modes, tiles, x_ref, d_ref, rates_ref, residues_ref, near_ref, far_ref, wide_ref, x_out, d_out, rate_out, coef_out, weight_out):
    rows = x_ref.shape[0]
    groups = LANES // width
    sq = (LANES, LANES)
    eye = iota(sq, 0) == iota(sq, 1)
    member = (iota(sq, 0) == iota(sq, 1) // width).astype(bf16)
    owner = iota((modes, LANES), 1) // width
    pick = iota((modes, LANES), 0) == iota((modes, LANES), 1) % width
    spot = iota(sq, 1).astype(f32)
    even = lax.axis_index("ctx") % 2 == 0
    pieces = rows // LANES
    gathered = []
    for k in range(tiles):
        group = (pl.program_id(0) * tiles + k) * groups
        home = pl.ds(pl.multiple_of(group // LANES * LANES, LANES), LANES)
        turn = (LANES - group % LANES) % LANES
        for ref in (rates_ref, residues_ref):
            value = pltpu.roll(ref[:, home], turn, 1)
            a = value.astype(bf16)
            rest = value - a.astype(f32)
            b = rest.astype(bf16)
            gathered += [a, b, (rest - b.astype(f32)).astype(bf16)]
    spread = mm(stack(gathered, 0), member)
    for k in range(tiles):
        here, lanes = slice(k * LANES, (k + 1) * LANES), lanes_of(k, tiles)
        parts = [spread[(6 * k + n) * modes : (6 * k + n + 1) * modes] for n in range(6)]
        wide, mixed = parts[0] + parts[1] + parts[2], parts[3] + parts[4] + parts[5]
        row = jnp.sum(jnp.where(pick, wide, 0.0), axis=0, keepdims=True)
        weight = jnp.sqrt(1.0 - jnp.exp(-2.0 * row))
        rate_out[:, lanes] = row
        weight_out[:, lanes] = weight
        coef_out[:, lanes] = jnp.sum(jnp.where(pick, mixed, 0.0), axis=0, keepdims=True) * weight
        wide_ref[:, lanes] = wide
        rate = column(row, eye)
        step = jnp.exp(-wide * float(LANES))
        got = []
        for power, src, out in ((LANES - 1.0 - spot, x_ref, x_out), (spot, d_ref, d_out)):
            high, low = split(jnp.exp(-rate * power))
            out[:, lanes] = src[:, here]
            flat = stack([src[h * LANES : (h + 1) * LANES, here] for h in range(pieces)], 1)
            full = mm(stack([high, low], 1), stack([flat, flat], 0))
            got.append([sel_rows(full[:, h * LANES : (h + 1) * LANES], modes, owner) for h in range(pieces)])
        end = got[0][0]
        for h in range(1, pieces):
            end = end * step + got[0][h]
        start = got[1][pieces - 1]
        for h in range(pieces - 2, -1, -1):
            start = start * step + got[1][h]
        near_ref[:, lanes] = jnp.where(even, end, start)
        far_ref[:, lanes] = jnp.where(even, start, end)


def local_kernel(width, modes, tiles, begin, *refs):
    x_ref, d_ref, rate_ref, wide_ref, coef_ref, skip_ref = refs[:6]
    yx_ref, yd_ref, sx_ref, sd_ref, grad_ref, far_ref, gskip_ref, own_ref = refs[-8:]
    rows = x_ref.shape[0]
    groups = LANES // width
    chunk = chunk_of(width, modes)
    fold = chunk // modes
    count = rows // chunk

    @pl.when(pl.program_id(0) == 0)
    def _():
        own_ref[...] = block_mask(width, modes)

    own = own_ref[...]
    owner = iota((chunk, LANES), 1) // width
    flat = (chunk, fold * LANES)
    t_int = iota(flat, 0)
    s_int = iota(flat, 1) // LANES * modes + iota(flat, 1) % modes
    spot = iota((chunk, LANES), 0).astype(f32)
    place = iota((modes, LANES), 1) % modes

    def spread(compact):
        return stack([compact] * groups, 0) * own

    def tall(compact):
        return stack([spread(compact[f * modes : (f + 1) * modes]) for f in range(fold)], 0)

    def broad(compact):
        return stack([spread(compact[:, f * LANES : (f + 1) * LANES]) for f in range(fold)], 1)

    def tables(lanes):
        row, coef, wide = rate_ref[:, lanes], coef_ref[:, lanes], wide_ref[:, lanes]
        down = jnp.exp(-row * spot)
        up = jnp.exp(row * spot)
        first = split(down * (coef * jnp.exp(row * (chunk - 1.0))))
        last = split(up * coef)
        start = split(stack([jnp.exp(-wide * (place + f * modes).astype(f32)) for f in range(fold)], 1))
        end = split(stack([jnp.exp(-wide * (chunk - 1 - f * modes - place).astype(f32)) for f in range(fold)], 1))
        forth = jnp.where(t_int >= s_int, three(*first, broad(end[0]), broad(end[1])), 0.0)
        back = jnp.where(t_int <= s_int, three(*last, broad(start[0]), broad(start[1])), 0.0)
        x_left = stack([*split(forth), *end], 0)
        d_left = stack([*split(back), *start], 0)
        return down, split(up), x_left, d_left

    def tiles_of(src, lanes):
        expanded = [tall(src[j * chunk : (j + 1) * chunk, lanes]) for j in range(count)]
        return [stack(expanded[j : j + 2], 1) for j in range(0, count, 2)]

    def near_part(left, right, src, dst, lanes):
        skip = skip_ref[:, lanes]
        found = []
        for p, block in enumerate(right):
            res = mm(left, block)
            own_part = halves(res[: 2 * chunk], chunk)
            ends = halves(res[2 * chunk :], modes)
            for q in range(2):
                half = slice(q * LANES, (q + 1) * LANES)
                spots = slice((2 * p + q) * chunk, (2 * p + q + 1) * chunk)
                dst[spots, lanes] = own_part[:, half] + skip * src[spots, lanes].astype(f32)
                found.append(ends[:, half])
        return found

    def near_grad(right, lanes):
        return lax.dot_general(
            stack([d_ref[j * chunk : (j + 1) * chunk, lanes] for j in range(count)], 1),
            stack(right, 1),
            (((1,), (1,)), ((), ())),
            preferred_element_type=f32,
        )

    def scans(ends_x, starts_d, lanes):
        wide = wide_ref[:, lanes]
        leap = jnp.exp(-wide * float(chunk))
        state = far = jnp.zeros((modes, LANES), f32)
        for j in range(count):
            sx_ref[j * modes : (j + 1) * modes, lanes] = state
            far = far + starts_d[j] * state
            state = (state + ends_x[j]) * leap
        far_ref[:, lanes] = far * jnp.exp(wide * float(chunk))
        state = jnp.zeros((modes, LANES), f32)
        for j in range(count - 1, -1, -1):
            sd_ref[j * modes : (j + 1) * modes, lanes] = state
            state = (state + starts_d[j]) * leap

    def skip_grad(lanes):
        total = jnp.zeros((chunk, LANES), f32)
        for j in range(count):
            spots = slice(j * chunk, (j + 1) * chunk)
            total = total + x_ref[spots, lanes].astype(f32) * d_ref[spots, lanes].astype(f32)
        gskip_ref[:, lanes] = jnp.sum(total, axis=0, keepdims=True)

    def finish_grad(pairs, down, up, lanes):
        parts = split(jnp.where(t_int >= s_int, pairs, 0.0))
        res = mm(stack(parts, 0), stack([tall(up[0]), tall(up[1])], 1))
        near = res[:chunk, :LANES] + res[:chunk, LANES:] + res[chunk:, :LANES]
        grad_ref[:, lanes] = jnp.sum(near * down, axis=0, keepdims=True)

    spans = [lanes_of(k, tiles, begin) for k in range(tiles)]
    ready = tables(spans[0])
    held = None
    for k, lanes in enumerate(spans):
        down, up, x_left, d_left = ready
        x_right = tiles_of(x_ref, lanes)
        ends_x = near_part(x_left, x_right, x_ref, yx_ref, lanes)
        pairs = near_grad(x_right, lanes)
        if k + 1 < tiles:
            ready = tables(spans[k + 1])
        starts_d = near_part(d_left, tiles_of(d_ref, lanes), d_ref, yd_ref, lanes)
        scans(ends_x, starts_d, lanes)
        skip_grad(lanes)
        if held is not None:
            finish_grad(*held)
        held = (pairs, down, up, lanes)
    finish_grad(*held)


def carry_grad_kernel(width, modes, scale, four, *refs):
    out_ref = refs[-1]
    near_ref, far_ref, rate_ref, weight_ref, skip_ref = refs[:5]
    p_ref, q_ref = refs[5:7]
    sq = (LANES, LANES)
    same = ((iota(sq, 0) // width) == (iota(sq, 1) // width)).astype(bf16)
    pick = iota((modes, LANES), 0) == iota((modes, LANES), 1) % modes
    place = lax.axis_index("ctx")
    inner = ((place == 1) | (place == 2)).astype(f32)
    middle = (place == 1).astype(f32)
    for k in range(p_ref.shape[1] // LANES):
        lanes = slice(k * LANES, (k + 1) * LANES)
        value = p_ref[:, lanes] * q_ref[:, lanes]
        if four:
            r_ref, s_ref = refs[7:9]
            value = value * inner + r_ref[:, lanes] * s_ref[:, lanes] * middle
        high, low = split(value + far_ref[:, lanes])
        sums = mm(stack([high, low], 1), stack([same, same], 0))
        far = jnp.sum(jnp.where(pick, sums, 0.0), axis=0, keepdims=True)
        out_ref[0:1, lanes] = (near_ref[:, lanes] + far * jnp.exp(-rate_ref[:, lanes])) * (weight_ref[:, lanes] * scale)
        out_ref[1:2, lanes] = skip_ref[:, lanes] * scale


def finish_kernel(width, modes, tiles, begin, forward, four, y_ref, held_ref, rate_ref, wide_ref, coef_ref, *refs):
    o_ref = refs[-1]
    rows = y_ref.shape[0]
    groups = LANES // width
    chunk = chunk_of(width, modes)
    count = rows // chunk
    own = block_mask(width, modes)
    spot = iota((chunk, LANES), 0).astype(f32)
    place = lax.axis_index("ctx")
    if not forward:
        place = 3 - place

    def spread(compact):
        return stack([compact] * groups, 0) * own

    for k in range(tiles):
        here, lanes = slice(k * LANES, (k + 1) * LANES), lanes_of(k, tiles, begin)
        row, coef, wide = rate_ref[:, lanes], coef_ref[:, lanes], wide_ref[:, lanes]
        leap = jnp.exp(-wide * float(chunk))
        state = refs[0][:, lanes]
        if four:
            both = state + refs[2][:, lanes] * jnp.exp(-wide * float(rows))
            state = jnp.where(place == 0, 0.0, jnp.where(place == 2, refs[1][:, lanes], both))
        table = coef * jnp.exp(row * ((chunk - 1.0) - spot if forward else spot))
        table = split(table)
        parts = [None] * count
        for j in range(count) if forward else range(count - 1, -1, -1):
            state = state * leap
            parts[j] = split(state + held_ref[j * modes : (j + 1) * modes, lanes])
        for p in range(0, count, 2):
            pair = parts[p : p + 2]
            res = three(*table, stack([spread(h) for h, _ in pair], 1), stack([spread(l) for _, l in pair], 1))
            for q in range(2):
                spots = slice((p + q) * chunk, (p + q + 1) * chunk)
                o_ref[spots, here] = (y_ref[spots, lanes] + res[:, q * LANES : (q + 1) * LANES]).astype(bf16)


def swap_states(near, far, power, even, count):
    end, start = jnp.where(even, near, far), jnp.where(even, far, near)
    before, after, prior, distance = end, start, None, 1
    have_x, have_d = None, None
    while distance < count:
        got_x = lax.ppermute(before, "ctx", [(i, i + distance) for i in range(count - distance)])
        got_d = lax.ppermute(after, "ctx", [(i + distance, i) for i in range(count - distance)])
        have_x = got_x if prior is None else have_x + prior * got_x
        have_d = got_d if prior is None else have_d + prior * got_d
        prior = power if prior is None else prior * power
        before, after = before + power * got_x, after + power * got_d
        power = power * power
        distance *= 2
    return have_x, have_d, start


def layer(inputs, cotangent, residues, decay_rates, skip_gain):
    local_batch, rows, channels = inputs.shape
    group_count, modes = residues.shape
    width = channels // group_count
    x, d = inputs.reshape(local_batch * rows, channels), cotangent.reshape(local_batch * rows, channels)
    rates, mixing = decay_rates.T, residues.T
    if group_count % LANES:
        rates, mixing = (jnp.pad(v, ((0, 0), (0, -group_count % LANES))) for v in (rates, mixing))
    skip = skip_gain.reshape(1, channels)
    count = lax.axis_size("ctx")
    four = count == 4
    blocks = channels // LANES
    every = pl.BlockSpec(memory_space=pl.ANY)
    params = pltpu.CompilerParams(vmem_limit_bytes=VMEM_LIMIT)

    whole = pl.BlockSpec(memory_space=pltpu.VMEM)

    def block(tiles, offset=0):
        return pl.BlockSpec((rows, tiles * LANES), lambda i: (0, i + offset))

    tiles = math.gcd(TILES_A, blocks)
    x, d = (pltpu.with_memory_space_constraint(value, pltpu.HBM) for value in (x, d))
    near, far, wide, x, d, rate, coef, weight = pl.pallas_call(
        functools.partial(ends_kernel, width, modes, tiles),
        grid=(blocks // tiles,),
        in_specs=[block(tiles), block(tiles), whole, whole],
        out_specs=[whole] * 8,
        out_shape=[jax.ShapeDtypeStruct((modes, channels), f32)] * 3
        + [jax.ShapeDtypeStruct((rows, channels), bf16)] * 2
        + [jax.ShapeDtypeStruct((1, channels), f32)] * 3,
        compiler_params=params,
        name="ends",
    )(x, d, rates, mixing)
    power = jnp.exp(-wide * float(rows))

    tiles_b = math.gcd(TILES_B, blocks)
    steps = blocks // tiles_b
    held = rows // chunk_of(width, modes) * modes

    def local(first, size, past):
        return pl.pallas_call(
            functools.partial(local_kernel, width, modes, tiles_b, first),
            grid=(size,),
            in_specs=[whole] * (6 if past is None else 13),
            out_specs=[whole] * 7,
            out_shape=[jax.ShapeDtypeStruct((rows, channels), f32)] * 2
            + [jax.ShapeDtypeStruct((size_of, channels), f32) for size_of in (held, held, 1, modes, 1)],
            scratch_shapes=[pltpu.VMEM((LANES, LANES), bf16)],
            input_output_aliases={} if past is None else {6 + n: n for n in range(7)},
            compiler_params=params,
            name="local",
        )(x, d, rate, wide, coef, skip, *(past or ()))

    def swap(value, pairs):
        return lax.ppermute(value, "ctx", pairs)

    if four:
        one = swap(near, [(0, 1), (1, 0), (2, 3), (3, 2)])
        cut_a, cut_b = max(1, steps * CUTS[0] // 16), max(2, steps * CUTS[1] // 16)
        past = local(0, cut_a, None)
        meet = far + power * one
        past, meet = lax.optimization_barrier((past, meet))
        two = swap(meet, [(1, 2), (2, 1)])
        past = local(cut_a, cut_b - cut_a, past)
        past, two = lax.optimization_barrier((past, two))
        three = swap(two, [(1, 0), (2, 3)])
        y_x, y_d, s_x, s_d, grad, far_grad, gskip = local(cut_b, steps - cut_b, past)
        states_x = states_d = (one, two, three)
        factors = (one, near, meet, two)
    else:
        even = lax.axis_index("ctx") % 2 == 0
        have_x, have_d, start = swap_states(near, far, power, even, count)
        y_x, y_d, s_x, s_d, grad, far_grad, gskip = local(0, steps, None)
        states_x, states_d = (have_x,), (have_d,)
        factors = (have_x, start)

    token_total = local_batch * rows * lax.axis_size("dp") * count
    grads = pl.pallas_call(
        functools.partial(carry_grad_kernel, width, modes, 1.0 / math.sqrt(token_total), four),
        in_specs=[pl.BlockSpec(memory_space=pltpu.VMEM)] * (5 + len(factors)),
        out_shape=jax.ShapeDtypeStruct((2, channels), f32),
        compiler_params=params,
        name="carry_grad",
    )(grad, far_grad, rate, weight, gskip, *factors)

    tiles_c = math.gcd(TILES_C, blocks)
    steps = blocks // tiles_c

    def finish(forward, first, size, past):
        y, inner, states = (y_x, s_x, states_x) if forward else (y_d, s_d, states_d)
        return pl.pallas_call(
            functools.partial(finish_kernel, width, modes, tiles_c, first, forward, four),
            grid=(size,),
            in_specs=[whole] * (5 + len(states)) + ([] if past is None else [every]),
            out_specs=block(tiles_c, first),
            out_shape=jax.ShapeDtypeStruct((rows, channels), bf16),
            input_output_aliases={} if past is None else {5 + len(states): 0},
            compiler_params=params,
            name="finish",
        )(y, inner, rate, wide, coef, *states, *(() if past is None else (past,)))

    results = {True: None, False: None}
    queue = [(True, 0, steps // 2), (True, steps // 2, steps - steps // 2)]
    queue += [(False, 0, steps // 2), (False, steps // 2, steps - steps // 2)]
    queue = [piece for piece in queue if piece[2] > 0]
    rounds = [("dp", k) for k in doubling(lax.axis_size("dp"))] + [("ctx", k) for k in doubling(count)]
    for axis, k in rounds:
        other = lax.ppermute(grads, axis, [(i, i ^ k) for i in range(lax.axis_size(axis))])
        if queue:
            forward, first, size = queue.pop(0)
            results[forward] = finish(forward, first, size, results[forward])
            results[forward], other = lax.optimization_barrier((results[forward], other))
        grads = grads + other
    for forward, first, size in queue:
        results[forward] = finish(forward, first, size, results[forward])
    return (
        results[True].reshape(inputs.shape),
        results[False].reshape(inputs.shape),
        grads[0].reshape(group_count, modes),
        grads[1],
    )


def doubling(size):
    return [1 << n for n in range(size.bit_length() - 1)]


def solution(mesh):
    placed = (P("dp", "ctx", "tp"), P("dp", "ctx", "tp"), P("tp", None), P("tp", None), P("tp"))
    return jax.shard_map(
        layer,
        mesh=mesh,
        in_specs=placed,
        out_specs=(P("dp", "ctx", "tp"), P("dp", "ctx", "tp"), P("tp", None), P("tp")),
        check_vma=False,
    )
```
